32 devices in a mesh: grp: 4 (over y, x), seq: 8 (over z, core).
Axes of the slice: x: 2, y: 2, z: 4, core: 2. Of those that a mesh axis runs over, the one named last changes fastest.
Arguments:
- owned_patches: bfloat16 [4, 1024, 1152], P('grp', 'seq'), may hold values from -6 to 6
- send_rows: int32 [4, 8, 128], P('grp', 'seq'), may hold values from 0 to 127, each once within a row
- receive_slot: int32 [4, 8, 128], P('grp', 'seq'), may hold values from 0 to 127, each once within a row
- segment_ids: int32 [4, 1024], P('grp', 'seq'), may hold values from 0 to 15, never falling along the last dimension, each value on 1 to 640 neighbouring positions
- class_label: int32 [4, 16], P('grp'), may hold values from 0 to 999
- drop_mask: int32 [4, 16], P('grp'), may hold values 0 or 1
- class_table: bfloat16 [1001, 1152], replicated, may hold values from -6 to 6
- modulation_weight: bfloat16 [1152, 3456], replicated, may hold values from -0.1875 to 0.1875
- attention_in: bfloat16 [1152, 1728], replicated, may hold values from -0.1875 to 0.1875
- attention_out: bfloat16 [576, 1152], replicated, may hold values from -0.25 to 0.25
- cotangent: bfloat16 [4, 1024, 1152], P('grp', 'seq'), may hold values from -6 to 6
Outputs:
- layer_output: bfloat16 [4, 1024, 1152], P('grp', 'seq')
- owner_gradient: bfloat16 [4, 1024, 1152], P('grp', 'seq')
- gradient_in: bfloat16 [1152, 1728], replicated
- gradient_out: bfloat16 [576, 1152], replicated
The draws below stay inside these ranges and needn't reach their ends.
Inputs may be any that keep to these rules, and one draw needn't show every extreme that they name: `send_rows`: for owner shard s of a group, entries 16 * d to 16 * d + 15 name, in slot order, the local rows that go to packed shard d; every local row once. `receive_slot`: packed row r of packed shard d takes slot c of what owner shard s sends to d, where the entry is 16 * s + c; every slot once. `segment_ids`: never falling along a group's tokens; every image has 1 to 640 tokens, one exactly 640.
All inputs are finite; a program needn't handle non-finite values. No bound on the sum of `drop_mask` on one device may be relied on, other than what follows from the above.
Results may differ from the reference program's by a relative error of at most 0.015.
Values may be sent and summed in bfloat16 or wider, within the bound.
A program may use at most 128 MiB of HBM per device.

```python
import math
import jax
import jax.numpy as jnp
import numpy as np
from jax import lax

D = 1152
HEADS = 8
HEAD = 72
ATT = 576
CLASSES = 1000
TOK_DEV = 128
IMAGES = 16
SEQ_TOK = 1024
MOST = 640
ALL_TOK = 4096
N_GRP = 4
N_SEQ = 8


def plant(array, own_key, smallest, top_value):
    index_at = [jax.random.randint(jax.random.fold_in(own_key, axis), (), 0, length) for axis, length in enumerate(array.shape)]
    widest = array.shape.index(max(array.shape))
    neighbour = index_at[:widest] + [(index_at[widest] + 1) % array.shape[widest]] + index_at[widest + 1:]
    return array.at[tuple(index_at)].set(smallest).at[tuple(neighbour)].set(top_value)


def level_of(rng, dims, split, low, top_value):
    def one(dim, shards_of):
        heights = jax.random.uniform(jax.random.fold_in(jax.random.fold_in(rng, 6), dim), (shards_of,), jnp.float32, low / len(split), top_value / len(split))
        return jnp.repeat(jnp.exp(heights), dims[dim] // shards_of).reshape((-1,) + (1,) * (len(dims) - dim - 1))

    level = one(*split[0])
    for cut in split[1:]:
        level = level * one(*cut)
    return level


def split_up(count, total, most, skew):
    portions = [(1 << 20) // math.isqrt(rank ** skew) + 1 for rank in range(2, count + 1)]
    surplus, counts = total - most - (count - 1), [1] * (count - 1)
    while surplus > 0:
        movable = [i for i in range(count - 1) if counts[i] < most]
        pool, left = sum([portions[i] for i in movable]), surplus
        for i in movable:
            extra = min(most - counts[i], max(1, left * portions[i] // pool), surplus)
            counts[i] = counts[i] + extra
            surplus = surplus - extra
    return np.array([most] + counts)


def uneven_parts(stream_key, amount, total, reach, lean):
    if amount == 2:
        one = jax.random.randint(stream_key, (), max(1, total - reach), min(reach, total - 1) + 1)
        return jnp.stack([one, total - one])
    tallies = jnp.asarray(split_up(amount, total, reach, lean), jnp.int32)
    pairs = (amount - 1) // 2
    source_of, receiver = tallies[1:1 + 2 * pairs:2], tallies[2:2 + 2 * pairs:2]
    room = jnp.minimum(source_of - 1, reach - receiver)
    passed = jax.random.randint(jax.random.fold_in(stream_key, 1), (pairs,), 0, 1 << 20) % (room + 1)
    tallies = tallies.at[1:1 + 2 * pairs:2].set(source_of - passed).at[2:2 + 2 * pairs:2].set(receiver + passed)
    return tallies[jax.random.permutation(jax.random.fold_in(stream_key, 2), amount)]


def bell_draw(stream_key, dims, deviation, reach, cuts=(), dtype=jnp.bfloat16):
    factor_of = level_of(stream_key, dims, cuts, -0.22, 0.18) if cuts else 1.0
    drawn = jax.random.normal(stream_key, dims, jnp.float32) * deviation * factor_of
    return jnp.minimum(jnp.maximum(drawn, -reach), reach).astype(dtype)


def setup_inputs(seed: int = 0) -> dict:
    key_list = jax.random.split(jax.random.key(seed), 12)
    owned_patches = bell_draw(key_list[0], (N_GRP, SEQ_TOK, D), 1.0, 6.0, ((0, 4), (1, 8)))
    send_rows = jax.vmap(lambda own: jax.random.permutation(own, TOK_DEV))(jax.random.split(key_list[1], N_GRP * N_SEQ)).reshape((N_GRP, N_SEQ, TOK_DEV)).astype(jnp.int32)
    receive_slot = jax.vmap(lambda own: jax.random.permutation(own, TOK_DEV))(jax.random.split(key_list[2], N_GRP * N_SEQ)).reshape((N_GRP, N_SEQ, TOK_DEV)).astype(jnp.int32)
    segment_ids = jax.vmap(lambda own: jnp.searchsorted(jnp.cumsum(uneven_parts(own, IMAGES, SEQ_TOK, MOST, 2)), jnp.arange(SEQ_TOK), side="right"))(jax.random.split(key_list[3], N_GRP)).reshape((N_GRP, SEQ_TOK)).astype(jnp.int32)
    class_label = plant(jax.random.randint(key_list[4], (N_GRP, IMAGES), 0, CLASSES), jax.random.fold_in(key_list[4], 1), 0, CLASSES - 1).astype(jnp.int32)
    drop_mask = plant((jax.random.randint(key_list[5], (N_GRP, IMAGES), 0, 10) < 1).astype(jnp.int32), jax.random.fold_in(key_list[5], 1), 0, 1)
    class_table = bell_draw(key_list[6], (CLASSES + 1, D), 1.0, 6.0)
    modulation_weight = bell_draw(key_list[7], (D, 3 * D), D ** -0.5, 0.1875)
    attention_in = bell_draw(key_list[8], (D, 3 * ATT), D ** -0.5, 0.1875)
    attention_out = bell_draw(key_list[9], (ATT, D), ATT ** -0.5, 0.25)
    cotangent = bell_draw(key_list[10], (N_GRP, SEQ_TOK, D), 1.0, 6.0, ((0, 4), (1, 8)))
    return dict(owned_patches=owned_patches, send_rows=send_rows, receive_slot=receive_slot, segment_ids=segment_ids, class_label=class_label, drop_mask=drop_mask, class_table=class_table, modulation_weight=modulation_weight, attention_in=attention_in, attention_out=attention_out, cotangent=cotangent)


EPSILON = 1e-06

def normalize(values):
    center = values - lax.optimization_barrier(jnp.mean(values, axis=-1, keepdims=True))
    spread = lax.optimization_barrier(jnp.mean(center * center, axis=-1, keepdims=True))
    inverse_spread = lax.rsqrt(spread + EPSILON)
    return (center * inverse_spread, inverse_spread)

def rounded(values):
    return lax.optimization_barrier(values.astype(jnp.bfloat16)).astype(jnp.float32)

def take_rows(table, positions):
    return jnp.take(table, positions, axis=0)

def place_rows(source, positions):
    return jnp.zeros_like(source).at[positions].set(source)

def to_packed(owned, send_rows, receive_slot):
    shards, per_shard = send_rows.shape
    slot_count = per_shard // shards
    feature_width = owned.shape[-1]
    by_owner = owned.reshape(shards, per_shard, feature_width)
    outgoing = jax.vmap(take_rows)(by_owner, send_rows)
    incoming = outgoing.reshape(shards, shards, slot_count, feature_width).transpose(1, 0, 2, 3)
    incoming = incoming.reshape(shards, per_shard, feature_width)
    return jax.vmap(take_rows)(incoming, receive_slot).reshape(shards * per_shard, feature_width)

def to_owners(packed_rows, send_rows, receive_slot):
    shards, per_shard = send_rows.shape
    slot_count = per_shard // shards
    feature_width = packed_rows.shape[-1]
    by_packed = packed_rows.reshape(shards, per_shard, feature_width)
    slotted = jax.vmap(place_rows)(by_packed, receive_slot)
    returned = slotted.reshape(shards, shards, slot_count, feature_width).transpose(1, 0, 2, 3)
    returned = returned.reshape(shards, per_shard, feature_width)
    return jax.vmap(place_rows)(returned, send_rows).reshape(shards * per_shard, feature_width)

def exponent(query_block, key_heads, image_query, image_keys):
    logits = jnp.einsum('qhe,khe->qhk', query_block, key_heads) * HEAD ** (-0.5)
    joined = (image_query[:, None] == image_keys[None, :])[:, None, :]
    return jnp.exp(jnp.where(joined, logits, -jnp.inf))

def group_forward(query_heads, key_heads, value_heads, images):
    total_rows = query_heads.shape[0]
    block_rows = math.gcd(total_rows, 512)
    block_count = total_rows // block_rows

    def one_block(pair):
        query_block, image_block = pair
        powers = exponent(query_block, key_heads, image_block, images)
        totals = lax.optimization_barrier(jnp.sum(powers, axis=-1))
        weighted = jnp.einsum('qhk,khe->qhe', rounded(powers), value_heads)
        return (weighted, totals)
    weighted, totals = lax.map(one_block, (query_heads.reshape(block_count, block_rows, HEADS, HEAD), images.reshape(block_count, block_rows)))
    return (weighted.reshape(total_rows, HEADS, HEAD), totals.reshape(total_rows, HEADS))

def group_backward(query_heads, key_heads, value_heads, cotangent_heads, images, totals, delta_rows):
    total_rows = query_heads.shape[0]
    block_rows = math.gcd(total_rows, 512)
    block_count = total_rows // block_rows

    def one_block(carried, pieces):
        query_block, cotangent_block, image_block, total_block, delta_block = pieces
        weights = exponent(query_block, key_heads, image_block, images) / total_block[:, :, None]
        weight_cotangent = jnp.einsum('qhe,khe->qhk', cotangent_block, value_heads)
        score_cotangent = rounded(weights * (weight_cotangent - delta_block[:, :, None]))
        query_part = jnp.einsum('qhk,khe->qhe', score_cotangent, key_heads)
        key_sum = carried[0] + jnp.einsum('qhk,qhe->khe', score_cotangent, query_block)
        value_sum = carried[1] + jnp.einsum('qhk,qhe->khe', rounded(weights), cotangent_block)
        return ((key_sum, value_sum), query_part)
    zeros_start = jnp.zeros(key_heads.shape, jnp.float32)
    pieces = (query_heads.reshape(block_count, block_rows, HEADS, HEAD), cotangent_heads.reshape(block_count, block_rows, HEADS, HEAD), images.reshape(block_count, block_rows), totals.reshape(block_count, block_rows, HEADS), delta_rows.reshape(block_count, block_rows, HEADS))
    (key_sum, value_sum), query_parts = lax.scan(one_block, (zeros_start, zeros_start), pieces)
    return (query_parts.reshape(total_rows, HEADS, HEAD), key_sum, value_sum)

def reference(owned_patches, send_rows, receive_slot, segment_ids, class_label, drop_mask, class_table, modulation_weight, attention_in, attention_out, cotangent):
    factor = HEAD ** (-0.5)
    outputs = []
    owner_rows = []
    in_total = jnp.zeros(attention_in.shape, jnp.float32)
    out_total = jnp.zeros(attention_out.shape, jnp.float32)
    for group in range(owned_patches.shape[0]):
        images = segment_ids[group]
        packed = to_packed(owned_patches[group], send_rows[group], receive_slot[group])
        chosen = jnp.where(drop_mask[group] == 1, CLASSES, class_label[group]).astype(jnp.int32)
        condition = jnp.take(class_table, chosen, axis=0)
        activated = jax.nn.silu(condition.astype(jnp.float32)).astype(jnp.bfloat16)
        modulation = jnp.dot(activated, modulation_weight, preferred_element_type=jnp.float32)
        per_token = jnp.take(modulation, images, axis=0)
        shift_rows = per_token[:, :D]
        scale_rows = per_token[:, D:2 * D]
        gate_rows = per_token[:, 2 * D:]
        row_values = packed.astype(jnp.float32)
        normed, inverse_spread = normalize(row_values)
        hidden = (normed * (1.0 + scale_rows) + shift_rows).astype(jnp.bfloat16)
        projected_f = jnp.dot(hidden, attention_in, preferred_element_type=jnp.float32)
        heads_all = rounded(projected_f).reshape(SEQ_TOK, 3, HEADS, HEAD)
        query_heads = heads_all[:, 0]
        key_heads = heads_all[:, 1]
        value_heads = heads_all[:, 2]
        weighted, totals = group_forward(query_heads, key_heads, value_heads, images)
        attended_f = (weighted / totals[:, :, None]).reshape(SEQ_TOK, ATT)
        attended = attended_f.astype(jnp.bfloat16)
        attended_heads = rounded(attended_f).reshape(SEQ_TOK, HEADS, HEAD)
        projected = jnp.dot(attended, attention_out, preferred_element_type=jnp.float32)
        outputs.append((row_values + gate_rows * projected).astype(jnp.bfloat16))
        upstream = cotangent[group].astype(jnp.float32)
        branch = (gate_rows * upstream).astype(jnp.bfloat16)
        out_total = out_total + jnp.dot(attended.T, branch, preferred_element_type=jnp.float32)
        attended_cot_f = jnp.dot(branch, attention_out.T, preferred_element_type=jnp.float32)
        cotangent_heads = rounded(attended_cot_f).reshape(SEQ_TOK, HEADS, HEAD)
        delta_rows = lax.optimization_barrier(jnp.sum(cotangent_heads * attended_heads, axis=-1))
        query_sum, key_sum, value_sum = group_backward(query_heads, key_heads, value_heads, cotangent_heads, images, totals, delta_rows)
        input_cotangent = jnp.concatenate([(query_sum * factor).reshape(SEQ_TOK, ATT).astype(jnp.bfloat16), (key_sum * factor).reshape(SEQ_TOK, ATT).astype(jnp.bfloat16), value_sum.reshape(SEQ_TOK, ATT).astype(jnp.bfloat16)], axis=1)
        in_total = in_total + jnp.dot(hidden.T, input_cotangent, preferred_element_type=jnp.float32)
        hidden_cotangent = jnp.dot(input_cotangent, attention_in.T, preferred_element_type=jnp.float32)
        scaled_cot = hidden_cotangent * (1.0 + scale_rows)
        packed_cotangent = upstream + inverse_spread * (scaled_cot - lax.optimization_barrier(jnp.mean(scaled_cot, axis=-1, keepdims=True)) - normed * lax.optimization_barrier(jnp.mean(scaled_cot * normed, axis=-1, keepdims=True)))
        owner_rows.append(to_owners(packed_cotangent.astype(jnp.bfloat16), send_rows[group], receive_slot[group]))
    norm_factor = ALL_TOK ** (-0.5)
    return (jnp.stack(outputs), jnp.stack(owner_rows), (in_total * norm_factor).astype(jnp.bfloat16), (out_total * norm_factor).astype(jnp.bfloat16))
```

```python
import functools
import math

import jax
import jax.numpy as jnp
from jax import lax
from jax.experimental import pallas as pl
from jax.experimental.pallas import tpu as pltpu
from jax.sharding import PartitionSpec as P

HEADS = 8
CLASSES = 1000


EPSILON = 1e-06
CONTRACT_LAST = (((1,), (1,)), ((), ()))


def normalize(values):
    center = values - jnp.mean(values, axis=-1, keepdims=True)
    spread = jnp.mean(center * center, axis=-1, keepdims=True)
    inverse_spread = lax.rsqrt(spread + EPSILON)
    return (center * inverse_spread, inverse_spread)


def exponent(query_heads, key_heads, image_query, image_keys, factor):
    logits = (
        jnp.einsum("qhe,khe->qhk", query_heads, key_heads, preferred_element_type=jnp.float32)
        * factor
    )
    joined = (image_query[:, None] == image_keys[None, :])[:, None, :]
    return jnp.exp(jnp.where(joined, logits, -jnp.inf))


def head_kernel(factor, block_rows, image_row, packed_ref, out_ref, flat_ref):
    shard_count, _, padded, tokens = packed_ref.shape
    total_rows = shard_count * tokens
    queries, keys, values, cotangents = (
        jnp.concatenate([packed_ref[s, part] for s in range(shard_count)], axis=1)
        for part in range(4)
    )
    key_columns = keys.T
    value_columns = values.T
    images = cotangents.astype(jnp.float32)[image_row : image_row + 8]
    image_column = images.T[:, :1]
    image_line = images[:1]
    key_sum = jnp.zeros((padded, total_rows), jnp.float32)
    value_sum = jnp.zeros((padded, total_rows), jnp.float32)
    attended_parts, query_parts = [], []
    for start in range(0, total_rows, block_rows):
        stop = start + block_rows
        query_block = queries[:, start:stop]
        cotangent_block = cotangents[:, start:stop]
        logits = jnp.dot(key_columns, query_block, preferred_element_type=jnp.float32)
        joined = image_column == image_line[:, start:stop]
        powers = jnp.where(joined, jnp.exp2(logits * (factor * math.log2(math.e))), 0.0)
        weights = powers * (1.0 / jnp.sum(powers, axis=0, keepdims=True))
        weights_low = weights.astype(jnp.bfloat16)
        attended = jnp.dot(values, weights_low, preferred_element_type=jnp.float32)
        attended_parts.append(attended.astype(jnp.bfloat16))
        attended_low = attended_parts[-1].astype(jnp.float32)
        delta = jnp.sum(
            cotangent_block.astype(jnp.float32) * attended_low, axis=0, keepdims=True
        )
        weight_cotangent = jnp.dot(
            value_columns, cotangent_block, preferred_element_type=jnp.float32
        )
        score_cotangent = (weights * (weight_cotangent - delta)).astype(jnp.bfloat16)
        query_parts.append(
            jnp.dot(keys, score_cotangent, preferred_element_type=jnp.float32) * factor
        )
        key_sum = key_sum + lax.dot_general(
            query_block, score_cotangent, CONTRACT_LAST, preferred_element_type=jnp.float32
        )
        value_sum = value_sum + lax.dot_general(
            cotangent_block, weights_low, CONTRACT_LAST, preferred_element_type=jnp.float32
        )
    results = (
        jnp.concatenate(attended_parts, axis=1),
        jnp.concatenate(query_parts, axis=1).astype(jnp.bfloat16),
        (key_sum * factor).astype(jnp.bfloat16),
        value_sum.astype(jnp.bfloat16),
    )
    for part, result in enumerate(results):
        flat_ref[part] = result
        for s in range(shard_count):
            out_ref[s, part] = result[:, s * tokens : (s + 1) * tokens]


def by_heads(hidden, attention_in, attention_out, branch, local_images, factor, scale):
    tokens = hidden.shape[0]
    head_width = attention_out.shape[0] // HEADS
    padded = -(-(head_width + 8) // 16) * 16
    projected = lax.dot_general(
        attention_in, hidden, (((0,), (1,)), ((), ())), preferred_element_type=jnp.float32
    ).astype(jnp.bfloat16)
    attended_cotangent = lax.dot_general(
        attention_out, branch, CONTRACT_LAST, preferred_element_type=jnp.float32
    ).astype(jnp.bfloat16)
    parts = jnp.concatenate([projected, attended_cotangent], axis=0)
    parts = parts.reshape(4, HEADS, head_width, tokens).transpose(1, 0, 2, 3)
    tail = jnp.zeros((1, 4, 1, 1), jnp.bfloat16).at[0, 3].set(1)
    tail = jnp.broadcast_to(
        tail * local_images.astype(jnp.bfloat16), (HEADS, 4, padded - head_width, tokens)
    )
    sent = jnp.concatenate([parts, tail], axis=2)
    heads = lax.all_to_all(sent, "seq", split_axis=0, concat_axis=0, tiled=True)
    total_rows = heads.shape[0] * tokens
    all_rows = lax.all_gather(
        jnp.concatenate([hidden, branch], axis=1), "seq", axis=0, tiled=True
    )
    results, flat = pl.pallas_call(
        functools.partial(head_kernel, factor, math.gcd(total_rows, 256), head_width),
        out_shape=(
            jax.ShapeDtypeStruct(heads.shape, jnp.bfloat16),
            jax.ShapeDtypeStruct((4, padded, total_rows), jnp.bfloat16),
        ),
        in_specs=[pl.BlockSpec(memory_space=pltpu.VMEM)],
        out_specs=(pl.BlockSpec(memory_space=pltpu.VMEM),) * 2,
    )(heads)
    model_width = hidden.shape[1]
    out_term = jnp.dot(
        flat[0, :head_width], all_rows[:, model_width:], preferred_element_type=jnp.float32
    )
    in_term = jnp.dot(
        flat[1:, :head_width].reshape(3 * head_width, total_rows),
        all_rows[:, :model_width],
        preferred_element_type=jnp.float32,
    )
    terms = jnp.concatenate([out_term, in_term], axis=0).astype(jnp.bfloat16)
    terms = lax.all_to_all(
        terms.reshape(4, head_width, model_width), "grp", split_axis=0, concat_axis=0, tiled=True
    )
    share = (jnp.sum(terms.astype(jnp.float32), axis=0) * scale).astype(jnp.bfloat16)
    joined = lax.all_gather(share, ("grp", "seq"), axis=0, tiled=True)
    inner_width = HEADS * head_width
    gradient_in = joined[inner_width:].T
    gradient_out = joined[:inner_width]
    returned = lax.all_to_all(results, "seq", split_axis=0, concat_axis=0, tiled=True)
    returned = returned[:, :, :head_width].transpose(1, 0, 2, 3)
    attended = returned[0].reshape(HEADS * head_width, tokens)
    input_cotangent = returned[1:].reshape(3 * HEADS * head_width, tokens)
    return attended, input_cotangent, gradient_in, gradient_out


def by_tokens(hidden, attention_in, attention_out, branch, local_images, factor, scale):
    tokens = hidden.shape[0]
    inner_width = attention_out.shape[0]
    head_width = inner_width // HEADS
    projected_in = jnp.dot(hidden, attention_in, preferred_element_type=jnp.float32).astype(
        jnp.bfloat16
    )
    queries = projected_in[:, :inner_width]
    key_value = projected_in[:, inner_width:]
    all_key_value, all_images = (
        lax.all_gather(key_value, "seq", axis=0, tiled=True),
        lax.all_gather(local_images, "seq", axis=0, tiled=True),
    )
    total_rows = all_key_value.shape[0]
    block_rows = math.gcd(total_rows, 512)
    block_count = total_rows // block_rows
    query_heads = queries.reshape(tokens, HEADS, head_width)

    def key_block(block_index):
        first_row = block_index * block_rows
        block_pair = lax.dynamic_slice_in_dim(all_key_value, first_row, block_rows, 0)
        block_images = lax.dynamic_slice_in_dim(all_images, first_row, block_rows, 0)
        key_heads = block_pair[:, :inner_width].reshape(block_rows, HEADS, head_width)
        value_heads = block_pair[:, inner_width:].reshape(block_rows, HEADS, head_width)
        return (key_heads, value_heads, block_images)

    def forward_step(block_index, carried):
        weighted, totals = carried
        key_heads, value_heads, block_images = key_block(block_index)
        powers = exponent(query_heads, key_heads, local_images, block_images, factor)
        totals = totals + jnp.sum(powers, axis=-1)
        weighted = weighted + jnp.einsum(
            "qhk,khe->qhe",
            powers.astype(jnp.bfloat16),
            value_heads,
            preferred_element_type=jnp.float32,
        )
        return (weighted, totals)

    start_state = (
        jnp.zeros((tokens, HEADS, head_width), jnp.float32),
        jnp.zeros((tokens, HEADS), jnp.float32),
    )
    weighted, totals = lax.fori_loop(0, block_count, forward_step, start_state)
    attended = (weighted / totals[:, :, None]).reshape(tokens, inner_width).astype(jnp.bfloat16)
    contract_last = (((1,), (1,)), ((), ()))
    attended_cotangent = lax.dot_general(
        branch, attention_out, contract_last, preferred_element_type=jnp.float32
    ).astype(jnp.bfloat16)
    cotangent_heads = attended_cotangent.reshape(tokens, HEADS, head_width)
    attended_heads = attended.reshape(tokens, HEADS, head_width)
    delta_rows = jnp.sum(
        cotangent_heads.astype(jnp.float32) * attended_heads.astype(jnp.float32), axis=-1
    )

    def query_step(block_index, carried):
        key_heads, value_heads, block_images = key_block(block_index)
        weights = (
            exponent(query_heads, key_heads, local_images, block_images, factor)
            / totals[:, :, None]
        )
        weight_cotangent = jnp.einsum(
            "qhe,khe->qhk", cotangent_heads, value_heads, preferred_element_type=jnp.float32
        )
        score_cotangent = (weights * (weight_cotangent - delta_rows[:, :, None])).astype(
            jnp.bfloat16
        )
        return carried + jnp.einsum(
            "qhk,khe->qhe", score_cotangent, key_heads, preferred_element_type=jnp.float32
        )

    query_sum = lax.fori_loop(
        0, block_count, query_step, jnp.zeros((tokens, HEADS, head_width), jnp.float32)
    )
    all_totals, all_delta = (
        lax.all_gather(totals, "seq", axis=0, tiled=True),
        lax.all_gather(delta_rows, "seq", axis=0, tiled=True),
    )
    local_keys = key_value[:, :inner_width].reshape(tokens, HEADS, head_width)
    local_values = key_value[:, inner_width:].reshape(tokens, HEADS, head_width)
    query_pair = jnp.concatenate([queries, attended_cotangent], axis=1)
    piece_rows = lax.all_gather(query_pair, "seq", axis=0, tiled=True)
    piece_images = lax.all_gather(local_images, "seq", axis=0, tiled=True)
    row_count = piece_rows.shape[0]
    piece_queries = piece_rows[:, :inner_width].reshape(row_count, HEADS, head_width)
    piece_cotangent = piece_rows[:, inner_width:].reshape(row_count, HEADS, head_width)
    weights = (
        exponent(piece_queries, local_keys, piece_images, local_images, factor)
        / all_totals[:, :, None]
    )
    weight_cotangent = jnp.einsum(
        "qhe,khe->qhk", piece_cotangent, local_values, preferred_element_type=jnp.float32
    )
    score_cotangent = (weights * (weight_cotangent - all_delta[:, :, None])).astype(jnp.bfloat16)
    key_part = jnp.einsum(
        "qhk,qhe->khe", score_cotangent, piece_queries, preferred_element_type=jnp.float32
    )
    value_part = jnp.einsum(
        "qhk,qhe->khe",
        weights.astype(jnp.bfloat16),
        piece_cotangent,
        preferred_element_type=jnp.float32,
    )
    key_sum = key_part.reshape(tokens, inner_width)
    value_sum = value_part.reshape(tokens, inner_width)
    input_cotangent = jnp.concatenate(
        [
            (query_sum * factor).reshape(tokens, inner_width).astype(jnp.bfloat16),
            (key_sum * factor).astype(jnp.bfloat16),
            value_sum.astype(jnp.bfloat16),
        ],
        axis=1,
    )
    out_weight_term = jnp.dot(attended.T, branch, preferred_element_type=jnp.float32)
    in_weight_term = jnp.dot(hidden.T, input_cotangent, preferred_element_type=jnp.float32)
    in_summed, out_summed = lax.psum((in_weight_term, out_weight_term), ("grp", "seq"))
    return (
        attended.T,
        input_cotangent.T,
        (in_summed * scale).astype(jnp.bfloat16),
        (out_summed * scale).astype(jnp.bfloat16),
    )


def shards(
    owned_patches,
    send_rows,
    receive_slot,
    segment_ids,
    class_label,
    drop_mask,
    class_table,
    modulation_weight,
    attention_in,
    attention_out,
    cotangent,
):
    shard_count = lax.axis_size("seq")
    tokens = owned_patches.shape[1]
    model_width = owned_patches.shape[2]
    inner_width = attention_out.shape[0]
    head_width = inner_width // HEADS
    factor = head_width ** (-0.5)
    outgoing = jnp.take(owned_patches[0], send_rows[0, 0], axis=0)
    incoming = lax.all_to_all(outgoing, "seq", split_axis=0, concat_axis=0, tiled=True)
    packed = jnp.take(incoming, receive_slot[0, 0], axis=0)
    chosen = jnp.where(drop_mask[0] == 1, CLASSES, class_label[0])
    condition = jnp.take(class_table, chosen, axis=0)
    activated = jax.nn.silu(condition.astype(jnp.float32)).astype(jnp.bfloat16)
    modulation = jnp.dot(activated, modulation_weight, preferred_element_type=jnp.float32)
    local_images = segment_ids[0]
    image_count = class_label.shape[1]
    one_hot = (local_images[:, None] == jnp.arange(image_count, dtype=jnp.int32)[None, :]).astype(
        jnp.float32
    )
    per_token = jnp.dot(
        one_hot, modulation, precision=lax.Precision.HIGHEST, preferred_element_type=jnp.float32
    )
    shift_rows = per_token[:, :model_width]
    scale_rows = per_token[:, model_width : 2 * model_width]
    gate_rows = per_token[:, 2 * model_width :]
    row_values = packed.astype(jnp.float32)
    normed, inverse_spread = normalize(row_values)
    hidden = (normed * (1.0 + scale_rows) + shift_rows).astype(jnp.bfloat16)
    upstream = cotangent[0].astype(jnp.float32)
    branch = (gate_rows * upstream).astype(jnp.bfloat16)
    norm_factor = (lax.axis_size("grp") * shard_count * tokens) ** (-0.5)
    split = by_heads if shard_count == HEADS and lax.axis_size("grp") == 4 else by_tokens
    attended, input_cotangent, gradient_in, gradient_out = split(
        hidden, attention_in, attention_out, branch, local_images, factor, norm_factor
    )
    projected = lax.dot_general(
        attended, attention_out, (((0,), (0,)), ((), ())), preferred_element_type=jnp.float32
    )
    layer_output = (row_values + gate_rows * projected).astype(jnp.bfloat16)
    hidden_cotangent = lax.dot_general(
        input_cotangent,
        attention_in,
        (((0,), (1,)), ((), ())),
        preferred_element_type=jnp.float32,
    )
    scaled_cot = hidden_cotangent * (1.0 + scale_rows)
    packed_cotangent = upstream + inverse_spread * (
        scaled_cot
        - jnp.mean(scaled_cot, axis=-1, keepdims=True)
        - normed * jnp.mean(scaled_cot * normed, axis=-1, keepdims=True)
    )
    packed_low = packed_cotangent.astype(jnp.bfloat16)
    back_order = jnp.zeros_like(packed_low).at[receive_slot[0, 0]].set(packed_low)
    returned = lax.all_to_all(back_order, "seq", split_axis=0, concat_axis=0, tiled=True)
    owner_gradient = jnp.zeros_like(returned).at[send_rows[0, 0]].set(returned)
    return (
        layer_output[None],
        owner_gradient[None],
        gradient_in,
        gradient_out,
    )


def solution(mesh):
    return jax.shard_map(
        shards,
        mesh=mesh,
        in_specs=(
            P("grp", "seq", None),
            P("grp", "seq", None),
            P("grp", "seq", None),
            P("grp", "seq"),
            P("grp", None),
            P("grp", None),
            P(),
            P(),
            P(),
            P(),
            P("grp", "seq", None),
        ),
        out_specs=(P("grp", "seq", None), P("grp", "seq", None), P(), P()),
        check_vma=False,
    )
```

```python
import functools
import math

import jax
import jax.numpy as jnp
from jax import lax
from jax.experimental import pallas as pl
from jax.experimental.pallas import tpu as pltpu
from jax.sharding import PartitionSpec as P

HEADS = 8
CLASSES = 1000


EPSILON = 1e-06
CONTRACT_LAST = (((1,), (1,)), ((), ()))


def normalize(values):
    center = values - jnp.mean(values, axis=-1, keepdims=True)
    spread = jnp.mean(center * center, axis=-1, keepdims=True)
    inverse_spread = lax.rsqrt(spread + EPSILON)
    return (center * inverse_spread, inverse_spread)


def exponent(query_heads, key_heads, image_query, image_keys, factor):
    logits = (
        jnp.einsum("qhe,khe->qhk", query_heads, key_heads, preferred_element_type=jnp.float32)
        * factor
    )
    joined = (image_query[:, None] == image_keys[None, :])[:, None, :]
    return jnp.exp(jnp.where(joined, logits, -jnp.inf))


def head_kernel(factor, block_rows, image_row, packed_ref, out_ref, flat_ref):
    shard_count, _, padded, tokens = packed_ref.shape
    total_rows = shard_count * tokens
    queries, keys, values, cotangents = (
        jnp.concatenate([packed_ref[s, part] for s in range(shard_count)], axis=1)
        for part in range(4)
    )
    key_columns = keys.T
    value_columns = values.T
    images = cotangents.astype(jnp.float32)[image_row : image_row + 8]
    image_column = images.T[:, :1]
    image_line = images[:1]
    key_sum = jnp.zeros((padded, total_rows), jnp.float32)
    value_sum = jnp.zeros((padded, total_rows), jnp.float32)
    attended_parts, query_parts = [], []
    for start in range(0, total_rows, block_rows):
        stop = start + block_rows
        query_block = queries[:, start:stop]
        cotangent_block = cotangents[:, start:stop]
        logits = jnp.dot(key_columns, query_block, preferred_element_type=jnp.float32)
        joined = image_column == image_line[:, start:stop]
        powers = jnp.where(joined, jnp.exp2(logits * (factor * math.log2(math.e))), 0.0)
        weights = powers * (1.0 / jnp.sum(powers, axis=0, keepdims=True))
        weights_low = weights.astype(jnp.bfloat16)
        attended = jnp.dot(values, weights_low, preferred_element_type=jnp.float32)
        attended_parts.append(attended.astype(jnp.bfloat16))
        attended_low = attended_parts[-1].astype(jnp.float32)
        delta = jnp.sum(
            cotangent_block.astype(jnp.float32) * attended_low, axis=0, keepdims=True
        )
        weight_cotangent = jnp.dot(
            value_columns, cotangent_block, preferred_element_type=jnp.float32
        )
        score_cotangent = (weights * (weight_cotangent - delta)).astype(jnp.bfloat16)
        query_parts.append(
            jnp.dot(keys, score_cotangent, preferred_element_type=jnp.float32) * factor
        )
        key_sum = key_sum + lax.dot_general(
            query_block, score_cotangent, CONTRACT_LAST, preferred_element_type=jnp.float32
        )
        value_sum = value_sum + lax.dot_general(
            cotangent_block, weights_low, CONTRACT_LAST, preferred_element_type=jnp.float32
        )
    results = (
        jnp.concatenate(attended_parts, axis=1),
        jnp.concatenate(query_parts, axis=1).astype(jnp.bfloat16),
        (key_sum * factor).astype(jnp.bfloat16),
        value_sum.astype(jnp.bfloat16),
    )
    for part, result in enumerate(results):
        flat_ref[part] = result
        for s in range(shard_count):
            out_ref[s, part] = result[:, s * tokens : (s + 1) * tokens]


def gather_kernel(share_ref, out_ref, local_sem, send_sems, recv_sems):
    group, place = lax.axis_index("grp"), lax.axis_index("seq")
    shard_count = out_ref.shape[0] // 4
    depth = shard_count // 2
    level, core = place // 2, place % 2
    groups = [group + bit - 2 * bit * ((group // bit) % 2) for bit in (1, 2)]
    groups.append(3 - group)

    def place_at(hop):
        return lax.rem(level + hop, depth) * 2 + core

    sideways = (groups[0], place)
    upward = (groups[1], place)
    partner = (group, level * 2 + 1 - core)
    along = [(group, place_at(hop)) for hop in range(1, depth)]
    barrier = pltpu.get_barrier_semaphore()
    for target in [sideways, upward, partner] + along:
        pl.semaphore_signal(
            barrier, inc=1, device_id=target, device_id_type=pl.DeviceIdType.MESH
        )
    pl.semaphore_wait(barrier, 3 + len(along))
    started = []

    def send(source, slot, target):
        copy = pltpu.make_async_remote_copy(
            src_ref=source,
            dst_ref=out_ref.at[slot],
            send_sem=send_sems.at[len(started)],
            recv_sem=recv_sems.at[slot],
            device_id=target,
            device_id_type=pl.DeviceIdType.MESH,
        )
        copy.start()
        started.append(copy)

    def arrive(slot):
        pltpu.make_async_remote_copy(
            src_ref=share_ref,
            dst_ref=out_ref.at[slot],
            send_sem=send_sems.at[0],
            recv_sem=recv_sems.at[slot],
            device_id=partner,
            device_id_type=pl.DeviceIdType.MESH,
        ).wait_recv()

    own = group * shard_count + place
    for target in along + [sideways, upward, partner]:
        send(share_ref, own, target)
    keep = pltpu.make_async_copy(share_ref, out_ref.at[own], local_sem)
    keep.start()
    for hop in range(depth):
        if hop:
            slot = group * shard_count + place_at(hop)
            arrive(slot)
            for target in (sideways, upward, partner):
                send(out_ref.at[slot], slot, target)
        for side, onward in ((0, upward), (1, sideways)):
            slot = groups[side] * shard_count + place_at(hop)
            arrive(slot)
            if hop % 2 == side:
                send(out_ref.at[slot], slot, onward)
            send(out_ref.at[slot], slot, partner)
    for hop in range(depth):
        slot = groups[2] * shard_count + place_at(hop)
        arrive(slot)
        send(out_ref.at[slot], slot, partner)
    for other in range(4):
        for step in range(depth):
            arrive(other * shard_count + step * 2 + 1 - core)
    keep.wait()
    for copy in started:
        copy.wait_send()


def gather_all(share):
    count = lax.axis_size("grp") * lax.axis_size("seq")
    gathered = pl.pallas_call(
        gather_kernel,
        out_shape=jax.ShapeDtypeStruct((count, *share.shape), share.dtype),
        in_specs=[pl.BlockSpec(memory_space=pltpu.VMEM)],
        out_specs=pl.BlockSpec(memory_space=pltpu.VMEM),
        scratch_shapes=[
            pltpu.SemaphoreType.DMA,
            pltpu.SemaphoreType.DMA((count,)),
            pltpu.SemaphoreType.DMA((count,)),
        ],
        compiler_params=pltpu.CompilerParams(collective_id=0, has_side_effects=True),
    )(share)
    return gathered.reshape(count * share.shape[0], share.shape[1])


def by_heads(hidden, attention_in, attention_out, branch, local_images, factor, scale):
    tokens = hidden.shape[0]
    head_width = attention_out.shape[0] // HEADS
    padded = -(-(head_width + 8) // 16) * 16
    projected = lax.dot_general(
        attention_in, hidden, (((0,), (1,)), ((), ())), preferred_element_type=jnp.float32
    ).astype(jnp.bfloat16)
    attended_cotangent = lax.dot_general(
        attention_out, branch, CONTRACT_LAST, preferred_element_type=jnp.float32
    ).astype(jnp.bfloat16)
    parts = jnp.concatenate([projected, attended_cotangent], axis=0)
    parts = parts.reshape(4, HEADS, head_width, tokens).transpose(1, 0, 2, 3)
    tail = jnp.zeros((1, 4, 1, 1), jnp.bfloat16).at[0, 3].set(1)
    tail = jnp.broadcast_to(
        tail * local_images.astype(jnp.bfloat16), (HEADS, 4, padded - head_width, tokens)
    )
    sent = jnp.concatenate([parts, tail], axis=2)
    heads = lax.all_to_all(sent, "seq", split_axis=0, concat_axis=0, tiled=True)
    total_rows = heads.shape[0] * tokens
    all_rows = lax.all_gather(
        jnp.concatenate([hidden, branch], axis=1), "seq", axis=0, tiled=True
    )
    results, flat = pl.pallas_call(
        functools.partial(head_kernel, factor, math.gcd(total_rows, 256), head_width),
        out_shape=(
            jax.ShapeDtypeStruct(heads.shape, jnp.bfloat16),
            jax.ShapeDtypeStruct((4, padded, total_rows), jnp.bfloat16),
        ),
        in_specs=[pl.BlockSpec(memory_space=pltpu.VMEM)],
        out_specs=(pl.BlockSpec(memory_space=pltpu.VMEM),) * 2,
    )(heads)
    model_width = hidden.shape[1]
    out_term = jnp.dot(
        flat[0, :head_width], all_rows[:, model_width:], preferred_element_type=jnp.float32
    )
    in_term = jnp.dot(
        flat[1:, :head_width].reshape(3 * head_width, total_rows),
        all_rows[:, :model_width],
        preferred_element_type=jnp.float32,
    )
    terms = jnp.concatenate([out_term, in_term], axis=0).astype(jnp.bfloat16)
    terms = lax.all_to_all(
        terms.reshape(4, head_width, model_width), "grp", split_axis=0, concat_axis=0, tiled=True
    )
    share = (jnp.sum(terms.astype(jnp.float32), axis=0) * scale).astype(jnp.bfloat16)
    joined = gather_all(share)
    inner_width = HEADS * head_width
    gradient_in = joined[inner_width:].T
    gradient_out = joined[:inner_width]
    returned = lax.all_to_all(results, "seq", split_axis=0, concat_axis=0, tiled=True)
    returned = returned[:, :, :head_width].transpose(1, 0, 2, 3)
    attended = returned[0].reshape(HEADS * head_width, tokens)
    input_cotangent = returned[1:].reshape(3 * HEADS * head_width, tokens)
    return attended, input_cotangent, gradient_in, gradient_out


def by_tokens(hidden, attention_in, attention_out, branch, local_images, factor, scale):
    tokens = hidden.shape[0]
    inner_width = attention_out.shape[0]
    head_width = inner_width // HEADS
    projected_in = jnp.dot(hidden, attention_in, preferred_element_type=jnp.float32).astype(
        jnp.bfloat16
    )
    queries = projected_in[:, :inner_width]
    key_value = projected_in[:, inner_width:]
    all_key_value, all_images = (
        lax.all_gather(key_value, "seq", axis=0, tiled=True),
        lax.all_gather(local_images, "seq", axis=0, tiled=True),
    )
    total_rows = all_key_value.shape[0]
    block_rows = math.gcd(total_rows, 512)
    block_count = total_rows // block_rows
    query_heads = queries.reshape(tokens, HEADS, head_width)

    def key_block(block_index):
        first_row = block_index * block_rows
        block_pair = lax.dynamic_slice_in_dim(all_key_value, first_row, block_rows, 0)
        block_images = lax.dynamic_slice_in_dim(all_images, first_row, block_rows, 0)
        key_heads = block_pair[:, :inner_width].reshape(block_rows, HEADS, head_width)
        value_heads = block_pair[:, inner_width:].reshape(block_rows, HEADS, head_width)
        return (key_heads, value_heads, block_images)

    def forward_step(block_index, carried):
        weighted, totals = carried
        key_heads, value_heads, block_images = key_block(block_index)
        powers = exponent(query_heads, key_heads, local_images, block_images, factor)
        totals = totals + jnp.sum(powers, axis=-1)
        weighted = weighted + jnp.einsum(
            "qhk,khe->qhe",
            powers.astype(jnp.bfloat16),
            value_heads,
            preferred_element_type=jnp.float32,
        )
        return (weighted, totals)

    start_state = (
        jnp.zeros((tokens, HEADS, head_width), jnp.float32),
        jnp.zeros((tokens, HEADS), jnp.float32),
    )
    weighted, totals = lax.fori_loop(0, block_count, forward_step, start_state)
    attended = (weighted / totals[:, :, None]).reshape(tokens, inner_width).astype(jnp.bfloat16)
    contract_last = (((1,), (1,)), ((), ()))
    attended_cotangent = lax.dot_general(
        branch, attention_out, contract_last, preferred_element_type=jnp.float32
    ).astype(jnp.bfloat16)
    cotangent_heads = attended_cotangent.reshape(tokens, HEADS, head_width)
    attended_heads = attended.reshape(tokens, HEADS, head_width)
    delta_rows = jnp.sum(
        cotangent_heads.astype(jnp.float32) * attended_heads.astype(jnp.float32), axis=-1
    )

    def query_step(block_index, carried):
        key_heads, value_heads, block_images = key_block(block_index)
        weights = (
            exponent(query_heads, key_heads, local_images, block_images, factor)
            / totals[:, :, None]
        )
        weight_cotangent = jnp.einsum(
            "qhe,khe->qhk", cotangent_heads, value_heads, preferred_element_type=jnp.float32
        )
        score_cotangent = (weights * (weight_cotangent - delta_rows[:, :, None])).astype(
            jnp.bfloat16
        )
        return carried + jnp.einsum(
            "qhk,khe->qhe", score_cotangent, key_heads, preferred_element_type=jnp.float32
        )

    query_sum = lax.fori_loop(
        0, block_count, query_step, jnp.zeros((tokens, HEADS, head_width), jnp.float32)
    )
    all_totals, all_delta = (
        lax.all_gather(totals, "seq", axis=0, tiled=True),
        lax.all_gather(delta_rows, "seq", axis=0, tiled=True),
    )
    local_keys = key_value[:, :inner_width].reshape(tokens, HEADS, head_width)
    local_values = key_value[:, inner_width:].reshape(tokens, HEADS, head_width)
    query_pair = jnp.concatenate([queries, attended_cotangent], axis=1)
    piece_rows = lax.all_gather(query_pair, "seq", axis=0, tiled=True)
    piece_images = lax.all_gather(local_images, "seq", axis=0, tiled=True)
    row_count = piece_rows.shape[0]
    piece_queries = piece_rows[:, :inner_width].reshape(row_count, HEADS, head_width)
    piece_cotangent = piece_rows[:, inner_width:].reshape(row_count, HEADS, head_width)
    weights = (
        exponent(piece_queries, local_keys, piece_images, local_images, factor)
        / all_totals[:, :, None]
    )
    weight_cotangent = jnp.einsum(
        "qhe,khe->qhk", piece_cotangent, local_values, preferred_element_type=jnp.float32
    )
    score_cotangent = (weights * (weight_cotangent - all_delta[:, :, None])).astype(jnp.bfloat16)
    key_part = jnp.einsum(
        "qhk,qhe->khe", score_cotangent, piece_queries, preferred_element_type=jnp.float32
    )
    value_part = jnp.einsum(
        "qhk,qhe->khe",
        weights.astype(jnp.bfloat16),
        piece_cotangent,
        preferred_element_type=jnp.float32,
    )
    key_sum = key_part.reshape(tokens, inner_width)
    value_sum = value_part.reshape(tokens, inner_width)
    input_cotangent = jnp.concatenate(
        [
            (query_sum * factor).reshape(tokens, inner_width).astype(jnp.bfloat16),
            (key_sum * factor).astype(jnp.bfloat16),
            value_sum.astype(jnp.bfloat16),
        ],
        axis=1,
    )
    out_weight_term = jnp.dot(attended.T, branch, preferred_element_type=jnp.float32)
    in_weight_term = jnp.dot(hidden.T, input_cotangent, preferred_element_type=jnp.float32)
    in_summed, out_summed = lax.psum((in_weight_term, out_weight_term), ("grp", "seq"))
    return (
        attended.T,
        input_cotangent.T,
        (in_summed * scale).astype(jnp.bfloat16),
        (out_summed * scale).astype(jnp.bfloat16),
    )


def shards(
    owned_patches,
    send_rows,
    receive_slot,
    segment_ids,
    class_label,
    drop_mask,
    class_table,
    modulation_weight,
    attention_in,
    attention_out,
    cotangent,
):
    shard_count = lax.axis_size("seq")
    tokens = owned_patches.shape[1]
    model_width = owned_patches.shape[2]
    inner_width = attention_out.shape[0]
    head_width = inner_width // HEADS
    factor = head_width ** (-0.5)
    outgoing = jnp.take(owned_patches[0], send_rows[0, 0], axis=0)
    incoming = lax.all_to_all(outgoing, "seq", split_axis=0, concat_axis=0, tiled=True)
    packed = jnp.take(incoming, receive_slot[0, 0], axis=0)
    chosen = jnp.where(drop_mask[0] == 1, CLASSES, class_label[0])
    condition = jnp.take(class_table, chosen, axis=0)
    activated = jax.nn.silu(condition.astype(jnp.float32)).astype(jnp.bfloat16)
    modulation = jnp.dot(activated, modulation_weight, preferred_element_type=jnp.float32)
    local_images = segment_ids[0]
    image_count = class_label.shape[1]
    one_hot = (local_images[:, None] == jnp.arange(image_count, dtype=jnp.int32)[None, :]).astype(
        jnp.float32
    )
    per_token = jnp.dot(
        one_hot, modulation, precision=lax.Precision.HIGHEST, preferred_element_type=jnp.float32
    )
    shift_rows = per_token[:, :model_width]
    scale_rows = per_token[:, model_width : 2 * model_width]
    gate_rows = per_token[:, 2 * model_width :]
    row_values = packed.astype(jnp.float32)
    normed, inverse_spread = normalize(row_values)
    hidden = (normed * (1.0 + scale_rows) + shift_rows).astype(jnp.bfloat16)
    upstream = cotangent[0].astype(jnp.float32)
    branch = (gate_rows * upstream).astype(jnp.bfloat16)
    norm_factor = (lax.axis_size("grp") * shard_count * tokens) ** (-0.5)
    split = by_heads if shard_count == HEADS and lax.axis_size("grp") == 4 else by_tokens
    attended, input_cotangent, gradient_in, gradient_out = split(
        hidden, attention_in, attention_out, branch, local_images, factor, norm_factor
    )
    projected = lax.dot_general(
        attended, attention_out, (((0,), (0,)), ((), ())), preferred_element_type=jnp.float32
    )
    layer_output = (row_values + gate_rows * projected).astype(jnp.bfloat16)
    hidden_cotangent = lax.dot_general(
        input_cotangent,
        attention_in,
        (((0,), (1,)), ((), ())),
        preferred_element_type=jnp.float32,
    )
    scaled_cot = hidden_cotangent * (1.0 + scale_rows)
    packed_cotangent = upstream + inverse_spread * (
        scaled_cot
        - jnp.mean(scaled_cot, axis=-1, keepdims=True)
        - normed * jnp.mean(scaled_cot * normed, axis=-1, keepdims=True)
    )
    packed_low = packed_cotangent.astype(jnp.bfloat16)
    back_order = jnp.zeros_like(packed_low).at[receive_slot[0, 0]].set(packed_low)
    returned = lax.all_to_all(back_order, "seq", split_axis=0, concat_axis=0, tiled=True)
    owner_gradient = jnp.zeros_like(returned).at[send_rows[0, 0]].set(returned)
    return (
        layer_output[None],
        owner_gradient[None],
        gradient_in,
        gradient_out,
    )


def solution(mesh):
    return jax.shard_map(
        shards,
        mesh=mesh,
        in_specs=(
            P("grp", "seq", None),
            P("grp", "seq", None),
            P("grp", "seq", None),
            P("grp", "seq"),
            P("grp", None),
            P("grp", None),
            P(),
            P(),
            P(),
            P(),
            P("grp", "seq", None),
        ),
        out_specs=(P("grp", "seq", None), P("grp", "seq", None), P(), P()),
        check_vma=False,
    )
```

```python
import functools
import math

import jax
import jax.numpy as jnp
from jax import lax
from jax.experimental import pallas as pl
from jax.experimental.pallas import tpu as pltpu
from jax.sharding import PartitionSpec as P

HEADS = 8
CLASSES = 1000


EPSILON = 1e-06
CONTRACT_LAST = (((1,), (1,)), ((), ()))


def normalize(values):
    center = values - jnp.mean(values, axis=-1, keepdims=True)
    spread = jnp.mean(center * center, axis=-1, keepdims=True)
    inverse_spread = lax.rsqrt(spread + EPSILON)
    return (center * inverse_spread, inverse_spread)


def exponent(query_heads, key_heads, image_query, image_keys, factor):
    logits = (
        jnp.einsum("qhe,khe->qhk", query_heads, key_heads, preferred_element_type=jnp.float32)
        * factor
    )
    joined = (image_query[:, None] == image_keys[None, :])[:, None, :]
    return jnp.exp(jnp.where(joined, logits, -jnp.inf))


def head_kernel(factor, block_rows, image_row, packed_ref, out_ref, flat_ref):
    shard_count, _, padded, tokens = packed_ref.shape
    total_rows = shard_count * tokens
    queries, keys, values, cotangents = (
        jnp.concatenate([packed_ref[s, part] for s in range(shard_count)], axis=1)
        for part in range(4)
    )
    key_columns = keys.T
    value_columns = values.T
    images = cotangents.astype(jnp.float32)[image_row : image_row + 8]
    image_column = images.T[:, :1]
    image_line = images[:1]
    key_sum = jnp.zeros((padded, total_rows), jnp.float32)
    value_sum = jnp.zeros((padded, total_rows), jnp.float32)
    attended_parts, query_parts = [], []
    for start in range(0, total_rows, block_rows):
        stop = start + block_rows
        query_block = queries[:, start:stop]
        cotangent_block = cotangents[:, start:stop]
        logits = jnp.dot(key_columns, query_block, preferred_element_type=jnp.float32)
        joined = image_column == image_line[:, start:stop]
        powers = jnp.where(joined, jnp.exp2(logits * (factor * math.log2(math.e))), 0.0)
        weights = powers * (1.0 / jnp.sum(powers, axis=0, keepdims=True))
        weights_low = weights.astype(jnp.bfloat16)
        attended = jnp.dot(values, weights_low, preferred_element_type=jnp.float32)
        attended_parts.append(attended.astype(jnp.bfloat16))
        attended_low = attended_parts[-1].astype(jnp.float32)
        delta = jnp.sum(
            cotangent_block.astype(jnp.float32) * attended_low, axis=0, keepdims=True
        )
        weight_cotangent = jnp.dot(
            value_columns, cotangent_block, preferred_element_type=jnp.float32
        )
        score_cotangent = (weights * (weight_cotangent - delta)).astype(jnp.bfloat16)
        query_parts.append(
            jnp.dot(keys, score_cotangent, preferred_element_type=jnp.float32) * factor
        )
        key_sum = key_sum + lax.dot_general(
            query_block, score_cotangent, CONTRACT_LAST, preferred_element_type=jnp.float32
        )
        value_sum = value_sum + lax.dot_general(
            cotangent_block, weights_low, CONTRACT_LAST, preferred_element_type=jnp.float32
        )
    results = (
        jnp.concatenate(attended_parts, axis=1),
        jnp.concatenate(query_parts, axis=1).astype(jnp.bfloat16),
        (key_sum * factor).astype(jnp.bfloat16),
        value_sum.astype(jnp.bfloat16),
    )
    for part, result in enumerate(results):
        flat_ref[part] = result
        for s in range(shard_count):
            out_ref[s, part] = result[:, s * tokens : (s + 1) * tokens]


def by_heads(
    hidden,
    attention_in,
    attention_out,
    branch,
    local_images,
    factor,
    scale,
    gate,
    gathered_cotangent,
):
    tokens, model_width = hidden.shape
    head_width = attention_out.shape[0] // HEADS
    padded = -(-(head_width + 8) // 16) * 16
    projected = lax.dot_general(
        attention_in, hidden, (((0,), (1,)), ((), ())), preferred_element_type=jnp.float32
    ).astype(jnp.bfloat16)
    attended_cotangent = lax.dot_general(
        attention_out, branch, CONTRACT_LAST, preferred_element_type=jnp.float32
    ).astype(jnp.bfloat16)
    parts = jnp.concatenate([projected, attended_cotangent], axis=0)
    parts = parts.reshape(4, HEADS, head_width, tokens).transpose(1, 0, 2, 3)
    tail = jnp.zeros((1, 4, 1, 1), jnp.bfloat16).at[0, 3].set(1)
    tail = jnp.broadcast_to(
        tail * local_images.astype(jnp.bfloat16), (HEADS, 4, padded - head_width, tokens)
    )
    sent = jnp.concatenate([parts, tail], axis=2)
    heads = lax.all_to_all(sent, "seq", split_axis=0, concat_axis=0, tiled=True)
    total_rows = heads.shape[0] * tokens
    all_hidden = lax.all_gather(hidden, "seq", axis=0, tiled=True)
    all_images = gathered_cotangent[:, model_width:]
    image_order = jnp.arange(gate.shape[0], dtype=jnp.int32).astype(jnp.bfloat16)
    one_hot = (all_images[:, :1] == image_order[None, :]).astype(jnp.float32)
    all_gates = jnp.dot(
        one_hot, gate, precision=lax.Precision.HIGHEST, preferred_element_type=jnp.float32
    )
    all_branch = (all_gates * gathered_cotangent[:, :model_width].astype(jnp.float32)).astype(
        jnp.bfloat16
    )
    results, flat = pl.pallas_call(
        functools.partial(head_kernel, factor, math.gcd(total_rows, 256), head_width),
        out_shape=(
            jax.ShapeDtypeStruct(heads.shape, jnp.bfloat16),
            jax.ShapeDtypeStruct((4, padded, total_rows), jnp.bfloat16),
        ),
        in_specs=[pl.BlockSpec(memory_space=pltpu.VMEM)],
        out_specs=(pl.BlockSpec(memory_space=pltpu.VMEM),) * 2,
    )(heads)
    out_term = jnp.dot(
        flat[0, :head_width], all_branch, preferred_element_type=jnp.float32
    )
    in_term = jnp.dot(
        flat[1:, :head_width].reshape(3 * head_width, total_rows),
        all_hidden,
        preferred_element_type=jnp.float32,
    )
    terms = jnp.concatenate([out_term, in_term], axis=0).astype(jnp.bfloat16)
    terms = lax.all_to_all(
        terms.reshape(4, head_width, model_width), "grp", split_axis=0, concat_axis=0, tiled=True
    )
    share = (jnp.sum(terms.astype(jnp.float32), axis=0) * scale).astype(jnp.bfloat16)
    joined = lax.all_gather(share, ("grp", "seq"), axis=0, tiled=True)
    inner_width = HEADS * head_width
    gradient_in = joined[inner_width:].T
    gradient_out = joined[:inner_width]
    returned = lax.all_to_all(results, "seq", split_axis=0, concat_axis=0, tiled=True)
    returned = returned[:, :, :head_width].transpose(1, 0, 2, 3)
    attended = returned[0].reshape(HEADS * head_width, tokens)
    input_cotangent = returned[1:].reshape(3 * HEADS * head_width, tokens)
    return attended, input_cotangent, gradient_in, gradient_out


def by_tokens(hidden, attention_in, attention_out, branch, local_images, factor, scale):
    tokens = hidden.shape[0]
    inner_width = attention_out.shape[0]
    head_width = inner_width // HEADS
    projected_in = jnp.dot(hidden, attention_in, preferred_element_type=jnp.float32).astype(
        jnp.bfloat16
    )
    queries = projected_in[:, :inner_width]
    key_value = projected_in[:, inner_width:]
    all_key_value, all_images = (
        lax.all_gather(key_value, "seq", axis=0, tiled=True),
        lax.all_gather(local_images, "seq", axis=0, tiled=True),
    )
    total_rows = all_key_value.shape[0]
    block_rows = math.gcd(total_rows, 512)
    block_count = total_rows // block_rows
    query_heads = queries.reshape(tokens, HEADS, head_width)

    def key_block(block_index):
        first_row = block_index * block_rows
        block_pair = lax.dynamic_slice_in_dim(all_key_value, first_row, block_rows, 0)
        block_images = lax.dynamic_slice_in_dim(all_images, first_row, block_rows, 0)
        key_heads = block_pair[:, :inner_width].reshape(block_rows, HEADS, head_width)
        value_heads = block_pair[:, inner_width:].reshape(block_rows, HEADS, head_width)
        return (key_heads, value_heads, block_images)

    def forward_step(block_index, carried):
        weighted, totals = carried
        key_heads, value_heads, block_images = key_block(block_index)
        powers = exponent(query_heads, key_heads, local_images, block_images, factor)
        totals = totals + jnp.sum(powers, axis=-1)
        weighted = weighted + jnp.einsum(
            "qhk,khe->qhe",
            powers.astype(jnp.bfloat16),
            value_heads,
            preferred_element_type=jnp.float32,
        )
        return (weighted, totals)

    start_state = (
        jnp.zeros((tokens, HEADS, head_width), jnp.float32),
        jnp.zeros((tokens, HEADS), jnp.float32),
    )
    weighted, totals = lax.fori_loop(0, block_count, forward_step, start_state)
    attended = (weighted / totals[:, :, None]).reshape(tokens, inner_width).astype(jnp.bfloat16)
    contract_last = (((1,), (1,)), ((), ()))
    attended_cotangent = lax.dot_general(
        branch, attention_out, contract_last, preferred_element_type=jnp.float32
    ).astype(jnp.bfloat16)
    cotangent_heads = attended_cotangent.reshape(tokens, HEADS, head_width)
    attended_heads = attended.reshape(tokens, HEADS, head_width)
    delta_rows = jnp.sum(
        cotangent_heads.astype(jnp.float32) * attended_heads.astype(jnp.float32), axis=-1
    )

    def query_step(block_index, carried):
        key_heads, value_heads, block_images = key_block(block_index)
        weights = (
            exponent(query_heads, key_heads, local_images, block_images, factor)
            / totals[:, :, None]
        )
        weight_cotangent = jnp.einsum(
            "qhe,khe->qhk", cotangent_heads, value_heads, preferred_element_type=jnp.float32
        )
        score_cotangent = (weights * (weight_cotangent - delta_rows[:, :, None])).astype(
            jnp.bfloat16
        )
        return carried + jnp.einsum(
            "qhk,khe->qhe", score_cotangent, key_heads, preferred_element_type=jnp.float32
        )

    query_sum = lax.fori_loop(
        0, block_count, query_step, jnp.zeros((tokens, HEADS, head_width), jnp.float32)
    )
    all_totals, all_delta = (
        lax.all_gather(totals, "seq", axis=0, tiled=True),
        lax.all_gather(delta_rows, "seq", axis=0, tiled=True),
    )
    local_keys = key_value[:, :inner_width].reshape(tokens, HEADS, head_width)
    local_values = key_value[:, inner_width:].reshape(tokens, HEADS, head_width)
    query_pair = jnp.concatenate([queries, attended_cotangent], axis=1)
    piece_rows = lax.all_gather(query_pair, "seq", axis=0, tiled=True)
    piece_images = lax.all_gather(local_images, "seq", axis=0, tiled=True)
    row_count = piece_rows.shape[0]
    piece_queries = piece_rows[:, :inner_width].reshape(row_count, HEADS, head_width)
    piece_cotangent = piece_rows[:, inner_width:].reshape(row_count, HEADS, head_width)
    weights = (
        exponent(piece_queries, local_keys, piece_images, local_images, factor)
        / all_totals[:, :, None]
    )
    weight_cotangent = jnp.einsum(
        "qhe,khe->qhk", piece_cotangent, local_values, preferred_element_type=jnp.float32
    )
    score_cotangent = (weights * (weight_cotangent - all_delta[:, :, None])).astype(jnp.bfloat16)
    key_part = jnp.einsum(
        "qhk,qhe->khe", score_cotangent, piece_queries, preferred_element_type=jnp.float32
    )
    value_part = jnp.einsum(
        "qhk,qhe->khe",
        weights.astype(jnp.bfloat16),
        piece_cotangent,
        preferred_element_type=jnp.float32,
    )
    key_sum = key_part.reshape(tokens, inner_width)
    value_sum = value_part.reshape(tokens, inner_width)
    input_cotangent = jnp.concatenate(
        [
            (query_sum * factor).reshape(tokens, inner_width).astype(jnp.bfloat16),
            (key_sum * factor).astype(jnp.bfloat16),
            value_sum.astype(jnp.bfloat16),
        ],
        axis=1,
    )
    out_weight_term = jnp.dot(attended.T, branch, preferred_element_type=jnp.float32)
    in_weight_term = jnp.dot(hidden.T, input_cotangent, preferred_element_type=jnp.float32)
    in_summed, out_summed = lax.psum((in_weight_term, out_weight_term), ("grp", "seq"))
    return (
        attended.T,
        input_cotangent.T,
        (in_summed * scale).astype(jnp.bfloat16),
        (out_summed * scale).astype(jnp.bfloat16),
    )


def shards(
    owned_patches,
    send_rows,
    receive_slot,
    segment_ids,
    class_label,
    drop_mask,
    class_table,
    modulation_weight,
    attention_in,
    attention_out,
    cotangent,
):
    shard_count = lax.axis_size("seq")
    tokens = owned_patches.shape[1]
    model_width = owned_patches.shape[2]
    inner_width = attention_out.shape[0]
    head_width = inner_width // HEADS
    factor = head_width ** (-0.5)
    split_heads = shard_count == HEADS and lax.axis_size("grp") == 4
    if split_heads:
        image_columns = jnp.broadcast_to(segment_ids[0][:, None], (tokens, 128))
        gathered_cotangent = lax.all_gather(
            jnp.concatenate([cotangent[0], image_columns.astype(jnp.bfloat16)], axis=1),
            "seq",
            axis=0,
            tiled=True,
        )
    outgoing = jnp.take(owned_patches[0], send_rows[0, 0], axis=0)
    incoming = lax.all_to_all(outgoing, "seq", split_axis=0, concat_axis=0, tiled=True)
    packed = jnp.take(incoming, receive_slot[0, 0], axis=0)
    chosen = jnp.where(drop_mask[0] == 1, CLASSES, class_label[0])
    condition = jnp.take(class_table, chosen, axis=0)
    activated = jax.nn.silu(condition.astype(jnp.float32)).astype(jnp.bfloat16)
    modulation = jnp.dot(activated, modulation_weight, preferred_element_type=jnp.float32)
    local_images = segment_ids[0]
    image_count = class_label.shape[1]
    one_hot = (local_images[:, None] == jnp.arange(image_count, dtype=jnp.int32)[None, :]).astype(
        jnp.float32
    )
    per_token = jnp.dot(
        one_hot, modulation, precision=lax.Precision.HIGHEST, preferred_element_type=jnp.float32
    )
    shift_rows = per_token[:, :model_width]
    scale_rows = per_token[:, model_width : 2 * model_width]
    gate_rows = per_token[:, 2 * model_width :]
    row_values = packed.astype(jnp.float32)
    normed, inverse_spread = normalize(row_values)
    hidden = (normed * (1.0 + scale_rows) + shift_rows).astype(jnp.bfloat16)
    upstream = cotangent[0].astype(jnp.float32)
    branch = (gate_rows * upstream).astype(jnp.bfloat16)
    norm_factor = (lax.axis_size("grp") * shard_count * tokens) ** (-0.5)
    common = (hidden, attention_in, attention_out, branch, local_images, factor, norm_factor)
    if split_heads:
        results = by_heads(*common, modulation[:, 2 * model_width :], gathered_cotangent)
    else:
        results = by_tokens(*common)
    attended, input_cotangent, gradient_in, gradient_out = results
    projected = lax.dot_general(
        attended, attention_out, (((0,), (0,)), ((), ())), preferred_element_type=jnp.float32
    )
    layer_output = (row_values + gate_rows * projected).astype(jnp.bfloat16)
    hidden_cotangent = lax.dot_general(
        input_cotangent,
        attention_in,
        (((0,), (1,)), ((), ())),
        preferred_element_type=jnp.float32,
    )
    scaled_cot = hidden_cotangent * (1.0 + scale_rows)
    packed_cotangent = upstream + inverse_spread * (
        scaled_cot
        - jnp.mean(scaled_cot, axis=-1, keepdims=True)
        - normed * jnp.mean(scaled_cot * normed, axis=-1, keepdims=True)
    )
    packed_low = packed_cotangent.astype(jnp.bfloat16)
    back_order = jnp.zeros_like(packed_low).at[receive_slot[0, 0]].set(packed_low)
    returned = lax.all_to_all(back_order, "seq", split_axis=0, concat_axis=0, tiled=True)
    owner_gradient = jnp.zeros_like(returned).at[send_rows[0, 0]].set(returned)
    return (
        layer_output[None],
        owner_gradient[None],
        gradient_in,
        gradient_out,
    )


def solution(mesh):
    return jax.shard_map(
        shards,
        mesh=mesh,
        in_specs=(
            P("grp", "seq", None),
            P("grp", "seq", None),
            P("grp", "seq", None),
            P("grp", "seq"),
            P("grp", None),
            P("grp", None),
            P(),
            P(),
            P(),
            P(),
            P("grp", "seq", None),
        ),
        out_specs=(P("grp", "seq", None), P("grp", "seq", None), P(), P()),
        check_vma=False,
    )
```

```python
import functools
import math

import jax
import jax.numpy as jnp
from jax import lax
from jax.experimental import pallas as pl
from jax.experimental.pallas import tpu as pltpu
from jax.sharding import PartitionSpec as P

HEADS = 8
CLASSES = 1000


EPSILON = 1e-06
CONTRACT_LAST = (((1,), (1,)), ((), ()))


def normalize(values):
    center = values - jnp.mean(values, axis=-1, keepdims=True)
    spread = jnp.mean(center * center, axis=-1, keepdims=True)
    inverse_spread = lax.rsqrt(spread + EPSILON)
    return (center * inverse_spread, inverse_spread)


def exponent(query_heads, key_heads, image_query, image_keys, factor):
    logits = (
        jnp.einsum("qhe,khe->qhk", query_heads, key_heads, preferred_element_type=jnp.float32)
        * factor
    )
    joined = (image_query[:, None] == image_keys[None, :])[:, None, :]
    return jnp.exp(jnp.where(joined, logits, -jnp.inf))


def head_kernel(factor, block_rows, image_row, packed_ref, out_ref, flat_ref):
    shard_count, _, padded, tokens = packed_ref.shape
    total_rows = shard_count * tokens
    queries, keys, values, cotangents = (
        jnp.concatenate([packed_ref[s, part] for s in range(shard_count)], axis=1)
        for part in range(4)
    )
    key_columns = keys.T
    value_columns = values.T
    images = cotangents.astype(jnp.float32)[image_row : image_row + 8]
    image_column = images.T[:, :1]
    image_line = images[:1]
    key_sum = jnp.zeros((padded, total_rows), jnp.float32)
    value_sum = jnp.zeros((padded, total_rows), jnp.float32)
    attended_parts, query_parts = [], []
    for start in range(0, total_rows, block_rows):
        stop = start + block_rows
        query_block = queries[:, start:stop]
        cotangent_block = cotangents[:, start:stop]
        logits = jnp.dot(key_columns, query_block, preferred_element_type=jnp.float32)
        joined = image_column == image_line[:, start:stop]
        powers = jnp.where(joined, jnp.exp2(logits * (factor * math.log2(math.e))), 0.0)
        weights = powers * (1.0 / jnp.sum(powers, axis=0, keepdims=True))
        weights_low = weights.astype(jnp.bfloat16)
        attended = jnp.dot(values, weights_low, preferred_element_type=jnp.float32)
        attended_parts.append(attended.astype(jnp.bfloat16))
        attended_low = attended_parts[-1].astype(jnp.float32)
        delta = jnp.sum(
            cotangent_block.astype(jnp.float32) * attended_low, axis=0, keepdims=True
        )
        weight_cotangent = jnp.dot(
            value_columns, cotangent_block, preferred_element_type=jnp.float32
        )
        score_cotangent = (weights * (weight_cotangent - delta)).astype(jnp.bfloat16)
        query_parts.append(
            jnp.dot(keys, score_cotangent, preferred_element_type=jnp.float32) * factor
        )
        key_sum = key_sum + lax.dot_general(
            query_block, score_cotangent, CONTRACT_LAST, preferred_element_type=jnp.float32
        )
        value_sum = value_sum + lax.dot_general(
            cotangent_block, weights_low, CONTRACT_LAST, preferred_element_type=jnp.float32
        )
    results = (
        jnp.concatenate(attended_parts, axis=1),
        jnp.concatenate(query_parts, axis=1).astype(jnp.bfloat16),
        (key_sum * factor).astype(jnp.bfloat16),
        value_sum.astype(jnp.bfloat16),
    )
    for part, result in enumerate(results):
        flat_ref[part] = result
        for s in range(shard_count):
            out_ref[s, part] = result[:, s * tokens : (s + 1) * tokens]


def gather_kernel(share_ref, out_ref, local_sem, send_sems, recv_sems):
    group, place = lax.axis_index("grp"), lax.axis_index("seq")
    shard_count = out_ref.shape[0] // 4
    depth = shard_count // 2
    level, core = place // 2, place % 2
    groups = [group + bit - 2 * bit * ((group // bit) % 2) for bit in (1, 2)]
    groups.append(3 - group)

    def place_at(hop):
        return lax.rem(level + hop, depth) * 2 + core

    sideways = (groups[0], place)
    upward = (groups[1], place)
    partner = (group, level * 2 + 1 - core)
    along = [(group, place_at(hop)) for hop in range(1, depth)]
    barrier = pltpu.get_barrier_semaphore()
    for target in [sideways, upward, partner] + along:
        pl.semaphore_signal(
            barrier, inc=1, device_id=target, device_id_type=pl.DeviceIdType.MESH
        )
    pl.semaphore_wait(barrier, 3 + len(along))
    started = []

    def send(source, slot, target):
        copy = pltpu.make_async_remote_copy(
            src_ref=source,
            dst_ref=out_ref.at[slot],
            send_sem=send_sems.at[len(started)],
            recv_sem=recv_sems.at[slot],
            device_id=target,
            device_id_type=pl.DeviceIdType.MESH,
        )
        copy.start()
        started.append(copy)

    def arrive(slot):
        pltpu.make_async_remote_copy(
            src_ref=share_ref,
            dst_ref=out_ref.at[slot],
            send_sem=send_sems.at[0],
            recv_sem=recv_sems.at[slot],
            device_id=partner,
            device_id_type=pl.DeviceIdType.MESH,
        ).wait_recv()

    own = group * shard_count + place
    for target in along + [sideways, upward, partner]:
        send(share_ref, own, target)
    keep = pltpu.make_async_copy(share_ref, out_ref.at[own], local_sem)
    keep.start()
    for hop in range(depth):
        if hop:
            slot = group * shard_count + place_at(hop)
            arrive(slot)
            for target in (sideways, upward, partner):
                send(out_ref.at[slot], slot, target)
        for side, onward in ((0, upward), (1, sideways)):
            slot = groups[side] * shard_count + place_at(hop)
            arrive(slot)
            if hop % 2 == side:
                send(out_ref.at[slot], slot, onward)
            send(out_ref.at[slot], slot, partner)
    for hop in range(depth):
        slot = groups[2] * shard_count + place_at(hop)
        arrive(slot)
        send(out_ref.at[slot], slot, partner)
    for other in range(4):
        for step in range(depth):
            arrive(other * shard_count + step * 2 + 1 - core)
    keep.wait()
    for copy in started:
        copy.wait_send()


def gather_all(share):
    count = lax.axis_size("grp") * lax.axis_size("seq")
    gathered = pl.pallas_call(
        gather_kernel,
        out_shape=jax.ShapeDtypeStruct((count, *share.shape), share.dtype),
        in_specs=[pl.BlockSpec(memory_space=pltpu.VMEM)],
        out_specs=pl.BlockSpec(memory_space=pltpu.VMEM),
        scratch_shapes=[
            pltpu.SemaphoreType.DMA,
            pltpu.SemaphoreType.DMA((count,)),
            pltpu.SemaphoreType.DMA((count,)),
        ],
        compiler_params=pltpu.CompilerParams(collective_id=0, has_side_effects=True),
    )(share)
    return gathered.reshape(count * share.shape[0], share.shape[1])


def by_heads(
    hidden,
    attention_in,
    attention_out,
    branch,
    local_images,
    factor,
    scale,
    gate,
    gathered_cotangent,
):
    tokens, model_width = hidden.shape
    head_width = attention_out.shape[0] // HEADS
    padded = -(-(head_width + 8) // 16) * 16
    projected = lax.dot_general(
        attention_in, hidden, (((0,), (1,)), ((), ())), preferred_element_type=jnp.float32
    ).astype(jnp.bfloat16)
    attended_cotangent = lax.dot_general(
        attention_out, branch, CONTRACT_LAST, preferred_element_type=jnp.float32
    ).astype(jnp.bfloat16)
    parts = jnp.concatenate([projected, attended_cotangent], axis=0)
    parts = parts.reshape(4, HEADS, head_width, tokens).transpose(1, 0, 2, 3)
    tail = jnp.zeros((1, 4, 1, 1), jnp.bfloat16).at[0, 3].set(1)
    tail = jnp.broadcast_to(
        tail * local_images.astype(jnp.bfloat16), (HEADS, 4, padded - head_width, tokens)
    )
    sent = jnp.concatenate([parts, tail], axis=2)
    heads = lax.all_to_all(sent, "seq", split_axis=0, concat_axis=0, tiled=True)
    total_rows = heads.shape[0] * tokens
    all_hidden = lax.all_gather(hidden, "seq", axis=0, tiled=True)
    all_images = gathered_cotangent[:, model_width:]
    image_order = jnp.arange(gate.shape[0], dtype=jnp.int32).astype(jnp.bfloat16)
    one_hot = (all_images[:, :1] == image_order[None, :]).astype(jnp.float32)
    all_gates = jnp.dot(
        one_hot, gate, precision=lax.Precision.HIGHEST, preferred_element_type=jnp.float32
    )
    all_branch = (all_gates * gathered_cotangent[:, :model_width].astype(jnp.float32)).astype(
        jnp.bfloat16
    )
    results, flat = pl.pallas_call(
        functools.partial(head_kernel, factor, math.gcd(total_rows, 256), head_width),
        out_shape=(
            jax.ShapeDtypeStruct(heads.shape, jnp.bfloat16),
            jax.ShapeDtypeStruct((4, padded, total_rows), jnp.bfloat16),
        ),
        in_specs=[pl.BlockSpec(memory_space=pltpu.VMEM)],
        out_specs=(pl.BlockSpec(memory_space=pltpu.VMEM),) * 2,
    )(heads)
    out_term = jnp.dot(
        flat[0, :head_width], all_branch, preferred_element_type=jnp.float32
    )
    in_term = jnp.dot(
        flat[1:, :head_width].reshape(3 * head_width, total_rows),
        all_hidden,
        preferred_element_type=jnp.float32,
    )
    terms = jnp.concatenate([out_term, in_term], axis=0).astype(jnp.bfloat16)
    terms = lax.all_to_all(
        terms.reshape(4, head_width, model_width), "grp", split_axis=0, concat_axis=0, tiled=True
    )
    share = (jnp.sum(terms.astype(jnp.float32), axis=0) * scale).astype(jnp.bfloat16)
    joined = gather_all(share)
    inner_width = HEADS * head_width
    gradient_in = joined[inner_width:].T
    gradient_out = joined[:inner_width]
    returned = lax.all_to_all(results, "seq", split_axis=0, concat_axis=0, tiled=True)
    returned = returned[:, :, :head_width].transpose(1, 0, 2, 3)
    attended = returned[0].reshape(HEADS * head_width, tokens)
    input_cotangent = returned[1:].reshape(3 * HEADS * head_width, tokens)
    return attended, input_cotangent, gradient_in, gradient_out


def by_tokens(hidden, attention_in, attention_out, branch, local_images, factor, scale):
    tokens = hidden.shape[0]
    inner_width = attention_out.shape[0]
    head_width = inner_width // HEADS
    projected_in = jnp.dot(hidden, attention_in, preferred_element_type=jnp.float32).astype(
        jnp.bfloat16
    )
    queries = projected_in[:, :inner_width]
    key_value = projected_in[:, inner_width:]
    all_key_value, all_images = (
        lax.all_gather(key_value, "seq", axis=0, tiled=True),
        lax.all_gather(local_images, "seq", axis=0, tiled=True),
    )
    total_rows = all_key_value.shape[0]
    block_rows = math.gcd(total_rows, 512)
    block_count = total_rows // block_rows
    query_heads = queries.reshape(tokens, HEADS, head_width)

    def key_block(block_index):
        first_row = block_index * block_rows
        block_pair = lax.dynamic_slice_in_dim(all_key_value, first_row, block_rows, 0)
        block_images = lax.dynamic_slice_in_dim(all_images, first_row, block_rows, 0)
        key_heads = block_pair[:, :inner_width].reshape(block_rows, HEADS, head_width)
        value_heads = block_pair[:, inner_width:].reshape(block_rows, HEADS, head_width)
        return (key_heads, value_heads, block_images)

    def forward_step(block_index, carried):
        weighted, totals = carried
        key_heads, value_heads, block_images = key_block(block_index)
        powers = exponent(query_heads, key_heads, local_images, block_images, factor)
        totals = totals + jnp.sum(powers, axis=-1)
        weighted = weighted + jnp.einsum(
            "qhk,khe->qhe",
            powers.astype(jnp.bfloat16),
            value_heads,
            preferred_element_type=jnp.float32,
        )
        return (weighted, totals)

    start_state = (
        jnp.zeros((tokens, HEADS, head_width), jnp.float32),
        jnp.zeros((tokens, HEADS), jnp.float32),
    )
    weighted, totals = lax.fori_loop(0, block_count, forward_step, start_state)
    attended = (weighted / totals[:, :, None]).reshape(tokens, inner_width).astype(jnp.bfloat16)
    contract_last = (((1,), (1,)), ((), ()))
    attended_cotangent = lax.dot_general(
        branch, attention_out, contract_last, preferred_element_type=jnp.float32
    ).astype(jnp.bfloat16)
    cotangent_heads = attended_cotangent.reshape(tokens, HEADS, head_width)
    attended_heads = attended.reshape(tokens, HEADS, head_width)
    delta_rows = jnp.sum(
        cotangent_heads.astype(jnp.float32) * attended_heads.astype(jnp.float32), axis=-1
    )

    def query_step(block_index, carried):
        key_heads, value_heads, block_images = key_block(block_index)
        weights = (
            exponent(query_heads, key_heads, local_images, block_images, factor)
            / totals[:, :, None]
        )
        weight_cotangent = jnp.einsum(
            "qhe,khe->qhk", cotangent_heads, value_heads, preferred_element_type=jnp.float32
        )
        score_cotangent = (weights * (weight_cotangent - delta_rows[:, :, None])).astype(
            jnp.bfloat16
        )
        return carried + jnp.einsum(
            "qhk,khe->qhe", score_cotangent, key_heads, preferred_element_type=jnp.float32
        )

    query_sum = lax.fori_loop(
        0, block_count, query_step, jnp.zeros((tokens, HEADS, head_width), jnp.float32)
    )
    all_totals, all_delta = (
        lax.all_gather(totals, "seq", axis=0, tiled=True),
        lax.all_gather(delta_rows, "seq", axis=0, tiled=True),
    )
    local_keys = key_value[:, :inner_width].reshape(tokens, HEADS, head_width)
    local_values = key_value[:, inner_width:].reshape(tokens, HEADS, head_width)
    query_pair = jnp.concatenate([queries, attended_cotangent], axis=1)
    piece_rows = lax.all_gather(query_pair, "seq", axis=0, tiled=True)
    piece_images = lax.all_gather(local_images, "seq", axis=0, tiled=True)
    row_count = piece_rows.shape[0]
    piece_queries = piece_rows[:, :inner_width].reshape(row_count, HEADS, head_width)
    piece_cotangent = piece_rows[:, inner_width:].reshape(row_count, HEADS, head_width)
    weights = (
        exponent(piece_queries, local_keys, piece_images, local_images, factor)
        / all_totals[:, :, None]
    )
    weight_cotangent = jnp.einsum(
        "qhe,khe->qhk", piece_cotangent, local_values, preferred_element_type=jnp.float32
    )
    score_cotangent = (weights * (weight_cotangent - all_delta[:, :, None])).astype(jnp.bfloat16)
    key_part = jnp.einsum(
        "qhk,qhe->khe", score_cotangent, piece_queries, preferred_element_type=jnp.float32
    )
    value_part = jnp.einsum(
        "qhk,qhe->khe",
        weights.astype(jnp.bfloat16),
        piece_cotangent,
        preferred_element_type=jnp.float32,
    )
    key_sum = key_part.reshape(tokens, inner_width)
    value_sum = value_part.reshape(tokens, inner_width)
    input_cotangent = jnp.concatenate(
        [
            (query_sum * factor).reshape(tokens, inner_width).astype(jnp.bfloat16),
            (key_sum * factor).astype(jnp.bfloat16),
            value_sum.astype(jnp.bfloat16),
        ],
        axis=1,
    )
    out_weight_term = jnp.dot(attended.T, branch, preferred_element_type=jnp.float32)
    in_weight_term = jnp.dot(hidden.T, input_cotangent, preferred_element_type=jnp.float32)
    in_summed, out_summed = lax.psum((in_weight_term, out_weight_term), ("grp", "seq"))
    return (
        attended.T,
        input_cotangent.T,
        (in_summed * scale).astype(jnp.bfloat16),
        (out_summed * scale).astype(jnp.bfloat16),
    )


def shards(
    owned_patches,
    send_rows,
    receive_slot,
    segment_ids,
    class_label,
    drop_mask,
    class_table,
    modulation_weight,
    attention_in,
    attention_out,
    cotangent,
):
    shard_count = lax.axis_size("seq")
    tokens = owned_patches.shape[1]
    model_width = owned_patches.shape[2]
    inner_width = attention_out.shape[0]
    head_width = inner_width // HEADS
    factor = head_width ** (-0.5)
    split_heads = shard_count == HEADS and lax.axis_size("grp") == 4
    if split_heads:
        image_columns = jnp.broadcast_to(segment_ids[0][:, None], (tokens, 128))
        gathered_cotangent = lax.all_gather(
            jnp.concatenate([cotangent[0], image_columns.astype(jnp.bfloat16)], axis=1),
            "seq",
            axis=0,
            tiled=True,
        )
    outgoing = jnp.take(owned_patches[0], send_rows[0, 0], axis=0)
    incoming = lax.all_to_all(outgoing, "seq", split_axis=0, concat_axis=0, tiled=True)
    packed = jnp.take(incoming, receive_slot[0, 0], axis=0)
    chosen = jnp.where(drop_mask[0] == 1, CLASSES, class_label[0])
    condition = jnp.take(class_table, chosen, axis=0)
    activated = jax.nn.silu(condition.astype(jnp.float32)).astype(jnp.bfloat16)
    modulation = jnp.dot(activated, modulation_weight, preferred_element_type=jnp.float32)
    local_images = segment_ids[0]
    image_count = class_label.shape[1]
    one_hot = (local_images[:, None] == jnp.arange(image_count, dtype=jnp.int32)[None, :]).astype(
        jnp.float32
    )
    per_token = jnp.dot(
        one_hot, modulation, precision=lax.Precision.HIGHEST, preferred_element_type=jnp.float32
    )
    shift_rows = per_token[:, :model_width]
    scale_rows = per_token[:, model_width : 2 * model_width]
    gate_rows = per_token[:, 2 * model_width :]
    row_values = packed.astype(jnp.float32)
    normed, inverse_spread = normalize(row_values)
    hidden = (normed * (1.0 + scale_rows) + shift_rows).astype(jnp.bfloat16)
    upstream = cotangent[0].astype(jnp.float32)
    branch = (gate_rows * upstream).astype(jnp.bfloat16)
    norm_factor = (lax.axis_size("grp") * shard_count * tokens) ** (-0.5)
    common = (hidden, attention_in, attention_out, branch, local_images, factor, norm_factor)
    if split_heads:
        results = by_heads(*common, modulation[:, 2 * model_width :], gathered_cotangent)
    else:
        results = by_tokens(*common)
    attended, input_cotangent, gradient_in, gradient_out = results
    projected = lax.dot_general(
        attended, attention_out, (((0,), (0,)), ((), ())), preferred_element_type=jnp.float32
    )
    layer_output = (row_values + gate_rows * projected).astype(jnp.bfloat16)
    hidden_cotangent = lax.dot_general(
        input_cotangent,
        attention_in,
        (((0,), (1,)), ((), ())),
        preferred_element_type=jnp.float32,
    )
    scaled_cot = hidden_cotangent * (1.0 + scale_rows)
    packed_cotangent = upstream + inverse_spread * (
        scaled_cot
        - jnp.mean(scaled_cot, axis=-1, keepdims=True)
        - normed * jnp.mean(scaled_cot * normed, axis=-1, keepdims=True)
    )
    packed_low = packed_cotangent.astype(jnp.bfloat16)
    back_order = jnp.zeros_like(packed_low).at[receive_slot[0, 0]].set(packed_low)
    returned = lax.all_to_all(back_order, "seq", split_axis=0, concat_axis=0, tiled=True)
    owner_gradient = jnp.zeros_like(returned).at[send_rows[0, 0]].set(returned)
    return (
        layer_output[None],
        owner_gradient[None],
        gradient_in,
        gradient_out,
    )


def solution(mesh):
    return jax.shard_map(
        shards,
        mesh=mesh,
        in_specs=(
            P("grp", "seq", None),
            P("grp", "seq", None),
            P("grp", "seq", None),
            P("grp", "seq"),
            P("grp", None),
            P("grp", None),
            P(),
            P(),
            P(),
            P(),
            P("grp", "seq", None),
        ),
        out_specs=(P("grp", "seq", None), P("grp", "seq", None), P(), P()),
        check_vma=False,
    )
```
